32 devices in a mesh: row: 8 (over z, x), col: 4 (over y, core).
Axes of the slice: x: 2, y: 2, z: 4, core: 2. Of those that a mesh axis runs over, the one named last changes fastest.
Arguments:
- features: bfloat16 [64, 4096], P(None, ('col', 'row')), may hold values from -4 to 4
- targets: float32 [128, 4096], P(None, ('col', 'row')), may hold values from -6 to 6
Outputs:
- coefficients: float32 [128, 4096], P(None, ('col', 'row'))
- residual: float32 [128, 4096], P(None, ('col', 'row'))
- direction: float32 [128, 4096], P(None, ('col', 'row'))
The draws below stay inside these ranges and needn't reach their ends.
All inputs are finite; a program needn't handle non-finite values.
Results may differ from the reference program's by a relative error of at most 0.0061.
Values may be sent and summed in bfloat16 or wider, within the bound.
No kernel may reach another device: no remote copies, remote signals or barrier semaphores. Data moves between devices by JAX's collectives and lax.ppermute only.
A program may use at most 64 MiB of HBM per device.

```python
import jax
import jax.numpy as jnp
from jax import lax

F = 64
R = 128
NS = 4096


def draw_features(key, part):
    values = jnp.clip(jax.random.normal(key, (F, NS), jnp.float32), -4.0, 4.0)
    return values.astype(jnp.bfloat16)


def level_of(own_key, extent, shards, least, largest):
    gain, own = 1.0, jax.random.fold_in(own_key, 6)
    for dim, shards_of in shards:
        draws = jnp.exp(jax.random.uniform(jax.random.fold_in(own, dim), (shards_of,), jnp.float32, least / len(shards), largest / len(shards)))
        gain = gain * jnp.repeat(draws, extent[dim] // shards_of).reshape([-1 if axis == dim else 1 for axis in range(len(extent))])
    return gain


def scatter_about(own_key, shape, deviation, most, pieces=(), kind=jnp.bfloat16):
    array = deviation * jax.random.normal(own_key, shape, jnp.float32)
    if pieces:
        array = array * level_of(own_key, shape, pieces, -0.22, 0.18)
    return jnp.clip(array, -most, most).astype(kind)


def setup_inputs(seed: int = 0) -> dict:
    streams_of = jax.random.split(jax.random.key(seed), 3)
    features = draw_features(jax.random.fold_in(streams_of[2], 71), 0)
    targets = scatter_about(streams_of[1], (R, NS), 1.0, 6.0, ((1, 32),), jnp.float32)
    return {"features": features, "targets": targets}


ridge_weight = 0.5
kernel_gain = 2.0
sharpness = 3.0

def kernel_rows(row_feat, row_sq, points, squares_all, panel_wide):
    inner = jnp.dot(row_feat.T, points, precision=lax.Precision.HIGHEST)
    distance = row_sq[:, None] + squares_all[None, :] - 2.0 * inner
    entries = jnp.exp(-sharpness * distance / F).astype(jnp.bfloat16)
    entries = lax.optimization_barrier(entries).astype(jnp.float32)
    return jnp.dot(panel_wide, entries.T, precision=lax.Precision.HIGHEST)

def gram(left, right):
    return lax.dot_general(left, right, (((1,), (1,)), ((), ())), precision=lax.Precision.HIGHEST)

def cholesky_factor(matrix):
    size = matrix.shape[0]
    index = jnp.arange(size, dtype=jnp.int32)

    def step(position, state):
        rest, factor = state
        pos = jnp.asarray(position).astype(jnp.int32)
        column = lax.dynamic_slice_in_dim(rest, pos, 1, 1)[:, 0]
        pivot = jnp.sqrt(lax.dynamic_slice_in_dim(column, pos, 1, 0)[0])
        column = jnp.where(index >= pos, column / pivot, jnp.zeros_like(column))
        rest = rest - column[:, None] * column[None, :]
        factor = lax.dynamic_update_slice_in_dim(factor, column[:, None], pos, 1)
        return (rest, factor)
    return lax.fori_loop(0, size, step, (matrix, jnp.zeros_like(matrix)))[1]

def solve_with(factor, rhs):
    size = factor.shape[0]

    def forward(position, solved):
        pos = jnp.asarray(position).astype(jnp.int32)
        line = lax.dynamic_slice_in_dim(factor, pos, 1, 0)
        pivot = lax.dynamic_slice_in_dim(line[0], pos, 1, 0)[0]
        value = (lax.dynamic_slice_in_dim(rhs, pos, 1, 0) - jnp.dot(line, solved, precision=lax.Precision.HIGHEST)) / pivot
        return lax.dynamic_update_slice_in_dim(solved, value, pos, 0)
    middle = lax.fori_loop(0, size, forward, jnp.zeros_like(rhs))

    def backward(step_count, solved):
        pos = (size - 1 - jnp.asarray(step_count)).astype(jnp.int32)
        line = lax.dynamic_slice_in_dim(factor, pos, 1, 1)
        pivot = lax.dynamic_slice_in_dim(line[:, 0], pos, 1, 0)[0]
        value = (lax.dynamic_slice_in_dim(middle, pos, 1, 0) - jnp.dot(line.T, solved, precision=lax.Precision.HIGHEST)) / pivot
        return lax.dynamic_update_slice_in_dim(solved, value, pos, 0)
    return lax.fori_loop(0, size, backward, jnp.zeros_like(rhs))

def reference(features, targets):
    points = features.astype(jnp.float32)
    squares_all = lax.optimization_barrier(jnp.sum(points * points, axis=0))
    panel = lax.optimization_barrier(targets.astype(jnp.bfloat16))
    panel_wide = panel.astype(jnp.float32)
    block_size = min(512, NS)
    blocks = NS // block_size
    row_blocks = points.reshape(F, blocks, block_size).transpose(1, 0, 2)
    sq_blocks = squares_all.reshape(blocks, block_size)

    def block_image(operands):
        return kernel_rows(operands[0], operands[1], points, squares_all, panel_wide)
    stacked = lax.map(block_image, (row_blocks, sq_blocks))
    kernel_image = stacked.transpose(1, 0, 2).reshape(R, NS)
    image = ridge_weight * targets + kernel_gain * kernel_image
    squares = gram(targets, targets)
    curvature = gram(targets, image)
    sym = 0.5 * (curvature + curvature.T)
    factor = cholesky_factor(sym)
    step_size = solve_with(factor, squares)
    coefficients = jnp.dot(step_size.T, targets, precision=lax.Precision.HIGHEST)
    residual = targets - jnp.dot(step_size.T, image, precision=lax.Precision.HIGHEST)
    conjugacy = gram(image, residual)
    correction = -solve_with(factor, conjugacy)
    direction = residual + jnp.dot(correction.T, targets, precision=lax.Precision.HIGHEST)
    return (coefficients, residual, direction)
```

```python
import jax
import jax.numpy as jnp
from jax import lax
from jax.experimental import pallas as pl
from jax.experimental.pallas import tpu as pltpu
from jax.sharding import PartitionSpec as P

ridge_weight = 0.5
kernel_gain = 2.0
sharpness = 3.0
log2_e = 1.4426950408889634
longest = 4096

f32 = jnp.float32
bf16 = jnp.bfloat16


def product_kernel(own_count, block, feat_rows, scale):
    def body(*refs):
        pieces = refs[:-6]
        z_ref, gram_ref, left, right, panel, stacked = refs[-6:]
        count = len(pieces)
        per_piece = pieces[0].shape[0]
        width = per_piece * block
        out_rows = pieces[0].shape[1] - feat_rows

        ones = jnp.ones((3, width), bf16)
        fill = jnp.zeros((10, width), bf16)
        for j, piece in enumerate(pieces):
            feat = jnp.concatenate([piece[b, :feat_rows, :] for b in range(per_piece)], axis=1)
            wide = feat.astype(f32)
            half = -0.5 * jnp.sum(wide * wide, axis=0, keepdims=True)
            high = half.astype(bf16)
            rest = half - high.astype(f32)
            mid = rest.astype(bf16)
            low = (rest - mid.astype(f32)).astype(bf16)
            norms = [high, mid, low]
            left[j * width : (j + 1) * width, :] = jnp.concatenate([feat] + norms + [ones, fill], axis=0).T
            if j < own_count:
                right[j] = jnp.concatenate([feat, ones] + norms + [fill], axis=0)
            for b in range(per_piece):
                panel[:, j * width + b * block : j * width + (b + 1) * block] = piece[b, feat_rows:, :]

        def entries_with(chunk, i):
            inner = jnp.dot(left[chunk, :], right[i], preferred_element_type=f32)
            return jnp.exp2(inner * (2.0 * scale * log2_e)).astype(bf16)

        def finish(i, cols, product):
            own_panel = panel[:, cols]
            z = product - own_panel.astype(f32)
            high = z.astype(bf16)
            stacked[:out_rows, cols] = own_panel
            stacked[out_rows : 2 * out_rows, cols] = high
            stacked[2 * out_rows :, cols] = (z - high.astype(f32)).astype(bf16)
            return z

        total = count * width
        if total <= longest:
            for i in range(own_count):
                product = jnp.dot(panel[...], entries_with(slice(None), i), preferred_element_type=f32)
                z = finish(i, slice(i * width, (i + 1) * width), product)
                if i == 0:
                    z_ref[...] = z[:, :block]
        else:

            def column(i, carry):
                def add(c, product):
                    start = pl.multiple_of(c * longest, longest)
                    chunk = pl.ds(start, longest)
                    return product + jnp.dot(panel[:, chunk], entries_with(chunk, i), preferred_element_type=f32)

                product = lax.fori_loop(0, total // longest, add, jnp.zeros((out_rows, width), f32))
                z = finish(i, pl.ds(pl.multiple_of(i * width, width), width), product)

                @pl.when(i == 0)
                def _():
                    z_ref[...] = z[:, :block]

                return carry

            lax.fori_loop(0, own_count, column, 0)
        sums = lax.dot_general(
            stacked[...], stacked[: 2 * out_rows, :], (((1,), (1,)), ((), ())), preferred_element_type=f32
        )
        r = out_rows
        cross = sums[2 * r :, r:]
        gram_ref[0] = sums[:r, :r]
        gram_ref[1] = sums[r : 2 * r, :r] + sums[2 * r :, :r]
        gram_ref[2] = sums[r : 2 * r, r:] + cross + cross.T

    return body


def lanes(v, k):
    return jnp.broadcast_to(v[:, k : k + 1], v.shape)


def rows(v, j):
    return jnp.broadcast_to(v[j : j + 1, :], v.shape)


def negated_inverse(a, size):
    groups = size // 8
    lane = lax.broadcasted_iota(jnp.int32, (8, size), 1)
    sub = lax.broadcasted_iota(jnp.int32, (8, size), 0)
    one_at = lambda mask: jnp.where(mask, 1.0, 0.0)
    for k in range(0, size, 2):
        q, j = divmod(k, 8)
        r0, r1 = rows(a[q], j), rows(a[q], j + 1)
        p, b, d = lanes(r0, k), lanes(r0, k + 1), lanes(r1, k + 1)
        scale = 1.0 / (p * d - b * b)
        r0 = r0 - one_at(lane == k)
        r1 = r1 - one_at(lane == k + 1)
        w0 = (d * r0 - b * r1) * scale
        w1 = (p * r1 - b * r0) * scale
        for i in range(groups):
            c0, c1 = lanes(a[i], k), lanes(a[i], k + 1)
            if i == q:
                c0 = c0 - one_at(sub == j)
                c1 = c1 - one_at(sub == j + 1)
            a[i] = a[i] - c0 * w0 - c1 * w1
        fix = ((lane == k) & (sub == j)) | ((lane == k + 1) & (sub == j + 1))
        a[q] = a[q] - 2.0 * one_at(fix)
    return a


def exact_dot(a, b):
    return jnp.dot(a, b, precision=lax.Precision.HIGHEST, preferred_element_type=f32)


def solve_kernel(mine, other, targets_ref, z_ref, coef_ref, res_ref, dir_ref):
    size = mine.shape[1]
    gram = mine[0] + other[0]
    mix_t = mine[1] + other[1]
    quad = mine[2] + other[2]
    diag = ridge_weight + kernel_gain
    mix = mix_t.T
    both = mix + mix_t
    half_gain = 0.5 * kernel_gain
    sym = diag * gram + half_gain * both
    outer = (diag * diag) * gram + (diag * kernel_gain) * both + (kernel_gain * kernel_gain) * quad
    curv = diag * gram + kernel_gain * mix
    eye = lax.broadcasted_iota(jnp.int32, (size, size), 0) == lax.broadcasted_iota(jnp.int32, (size, size), 1)
    on_diag = jnp.where(eye, sym, 0.0)
    by_col = lax.rsqrt(jnp.sum(on_diag, axis=0, keepdims=True))
    by_row = lax.rsqrt(jnp.sum(on_diag, axis=1, keepdims=True))
    unit = sym * by_row * by_col
    parts = negated_inverse([unit[8 * i : 8 * i + 8, :] for i in range(size // 8)], size)
    minus_inverse = jnp.concatenate(parts, axis=0) * by_row * by_col
    step_t = -exact_dot(gram, minus_inverse)
    correction_t = exact_dot(curv - exact_dot(step_t, outer), minus_inverse)
    targets = targets_ref[...]
    image = ridge_weight * targets + kernel_gain * (targets.astype(bf16).astype(f32) + z_ref[...])
    residual = targets - exact_dot(step_t, image)
    coef_ref[...] = exact_dot(step_t, targets)
    res_ref[...] = residual
    dir_ref[...] = residual + exact_dot(correction_t, targets)


def flips(size, bit):
    return [(i, i ^ bit) for i in range(size)]


def local(row_size, col_size):
    def run(features, targets):
        feat_rows, block = features.shape
        out_rows = targets.shape[0]
        payload = jnp.concatenate([features, targets.astype(bf16)], axis=0)[None]

        def flip(axis, bit):
            size = row_size if axis == "row" else col_size
            return lambda x: lax.ppermute(x, axis, flips(size, bit))

        hops = [("row", 1 << s) for s in reversed(range(1, row_size.bit_length() - 1))]
        hops += [("col", 1 << s) for s in reversed(range(1, col_size.bit_length() - 2))]
        pieces = [payload]
        for axis, bit in hops:
            got = [flip(axis, bit)(x) for x in pieces]
            if len(pieces) == 1 and pieces[0].shape[0] == 1:
                pieces = [jnp.concatenate([pieces[0], got[0]], axis=0)]
            else:
                pieces = pieces + got
        over_x, over_y = flip("row", 1), flip("col", col_size // 2)
        from_x = [over_x(x) for x in pieces]
        from_y = [over_y(x) for x in pieces]
        half = len(pieces) // 2
        far = [over_x(y) for y in from_y[:half]] + [over_y(x) for x in from_x[half:]]
        own = pieces + from_x + from_y + far
        partner = flip("col", 1)
        others = [partner(x) for x in own]

        width = own[0].shape[0] * block
        z, grams = pl.pallas_call(
            product_kernel(len(own), block, feat_rows, sharpness / feat_rows),
            out_shape=(
                jax.ShapeDtypeStruct((out_rows, block), f32),
                jax.ShapeDtypeStruct((3, out_rows, out_rows), f32),
            ),
            scratch_shapes=[
                pltpu.VMEM((2 * len(own) * width, feat_rows + 16), bf16),
                pltpu.VMEM((len(own), feat_rows + 16, width), bf16),
                pltpu.VMEM((out_rows, 2 * len(own) * width), bf16),
                pltpu.VMEM((3 * out_rows, len(own) * width), bf16),
            ],
        )(*own, *others)
        return pl.pallas_call(
            solve_kernel,
            out_shape=tuple(jax.ShapeDtypeStruct(targets.shape, f32) for _ in range(3)),
        )(grams, partner(grams), targets, z)

    return run


def solution(mesh):
    spec = P(None, ("col", "row"))
    return jax.shard_map(
        local(mesh.shape["row"], mesh.shape["col"]),
        mesh=mesh,
        in_specs=(spec, spec),
        out_specs=(spec, spec, spec),
        check_vma=False,
    )
```

```python
import jax
import jax.numpy as jnp
from jax import lax
from jax.experimental import pallas as pl
from jax.experimental.pallas import tpu as pltpu
from jax.sharding import PartitionSpec as P

ridge_weight = 0.5
kernel_gain = 2.0
sharpness = 3.0
log2_e = 1.4426950408889634
longest = 4096
widest = 512
step_rows = 2048
product_vmem = 28 << 20
solve_vmem = 4 << 20

f32 = jnp.float32
bf16 = jnp.bfloat16


def product_kernel(columns, feat_rows, scale, finish):
    def body(*refs):
        if finish:
            *pieces, part_ref, z_ref, gram_ref, left, right, panel, sums = refs
        else:
            *pieces, part_ref, left, right, panel = refs
        per_piece, payload_rows, block = pieces[0].shape
        width = per_piece * block
        out_rows = payload_rows - feat_rows
        sub = min(width, widest)

        ones = jnp.ones((3, block), bf16)
        fill = jnp.zeros((10, block), bf16)
        used = [c[0] for c in columns]

        def prepare(j, b):
            at = j * width + b * block
            if not isinstance(b, int):
                at = pl.multiple_of(at, block)
            here = pl.ds(at, block)
            feat = pieces[j][b, :feat_rows, :]
            wide = feat.astype(f32)
            half = -0.5 * jnp.sum(wide * wide, axis=0, keepdims=True)
            high = half.astype(bf16)
            rest = half - high.astype(f32)
            mid = rest.astype(bf16)
            low = (rest - mid.astype(f32)).astype(bf16)
            norms = [high, mid, low]
            left[here, :] = jnp.concatenate([feat] + norms + [ones, fill], axis=0).T
            if j in used:
                right[:, here] = jnp.concatenate([feat, ones] + norms + [fill], axis=0)
            panel[:, here] = pieces[j][b, feat_rows:, :]

        for j in range(len(pieces)):
            if width <= widest:
                for b in range(per_piece):
                    prepare(j, b)
            else:
                lax.fori_loop(0, per_piece, lambda b, carry, j=j: (prepare(j, b), carry)[1], 0)

        def product(here, cols):
            inner = jnp.dot(left[here, :], right[:, cols], preferred_element_type=f32)
            entries = jnp.exp2(inner * (2.0 * scale * log2_e)).astype(bf16)
            return jnp.dot(panel[:, here], entries, preferred_element_type=f32)

        if finish:
            sums[...] = jnp.zeros(sums.shape, f32)

        def column(n, s):
            piece, first, last = columns[n]
            static = isinstance(s, int)
            at, to = piece * width + s * sub, n * width + s * sub
            if not static:
                at, to = pl.multiple_of(at, sub), pl.multiple_of(to, sub)
            cols = pl.ds(at, sub)
            if (last - first) * width <= longest:
                total = product(pl.ds(first * width, (last - first) * width), cols)
            else:
                steps = (last - first) * width // step_rows

                def add(t, carry):
                    start = pl.multiple_of(first * width + t * step_rows, step_rows)
                    return carry + product(pl.ds(start, step_rows), cols)

                total = lax.fori_loop(0, steps, add, jnp.zeros((out_rows, sub), f32))
            if not finish:
                part_ref[:, pl.ds(to, sub)] = total
                return
            if n * width < part_ref.shape[1]:
                total = total + part_ref[:, pl.ds(to, sub)]
            own_panel = panel[:, cols]
            z = total - own_panel.astype(f32)
            if n == 0:
                if static:
                    if s == 0:
                        z_ref[...] = z[:, :block]
                else:

                    @pl.when(s == 0)
                    def _():
                        z_ref[...] = z[:, :block]

            high = z.astype(bf16)
            low = (z - high.astype(f32)).astype(bf16)
            rhs = jnp.concatenate([own_panel, high], axis=0)
            lhs = jnp.concatenate([rhs, low], axis=0)
            sums[...] += lax.dot_general(lhs, rhs, (((1,), (1,)), ((), ())), preferred_element_type=f32)

        for n in range(len(columns)):
            if width == sub:
                column(n, 0)
            else:
                lax.fori_loop(0, width // sub, lambda s, carry, n=n: (column(n, s), carry)[1], 0)

        if finish:
            r = out_rows
            cross = sums[2 * r :, r:]
            gram_ref[0] = sums[:r, :r]
            gram_ref[1] = sums[r : 2 * r, :r] + sums[2 * r :, :r]
            gram_ref[2] = sums[r : 2 * r, r:] + cross + cross.T

    return body


def lanes(v, k):
    return jnp.broadcast_to(v[:, k : k + 1], v.shape)


def rows(v, j):
    return jnp.broadcast_to(v[j : j + 1, :], v.shape)


def negated_inverse(a, size):
    groups = size // 8
    lane = lax.broadcasted_iota(jnp.int32, (8, size), 1)
    sub = lax.broadcasted_iota(jnp.int32, (8, size), 0)

    def one_at(mask):
        return jnp.where(mask, 1.0, 0.0)

    one = one_at(lane >= 0)
    for q in range(groups):
        r = a[q]
        c = [lanes(r, 8 * q + m) * one for m in range(8)]
        for j in range(0, 8, 2):
            k = 8 * q + j
            p, b, d = rows(c[j], j), rows(c[j + 1], j), rows(c[j + 1], j + 1)
            scale = 1.0 / (p * d - b * b)
            c0 = c[j] - one_at(sub == j)
            c1 = c[j + 1] - one_at(sub == j + 1)
            u0 = (c0 * d - c1 * b) * scale
            u1 = (c1 * p - c0 * b) * scale
            for m in range(j + 2, 8):
                c[m] = c[m] - (u0 * rows(c[m], j) + u1 * rows(c[m], j + 1))
            fix = 2.0 * one_at(((lane == k) & (sub == j)) | ((lane == k + 1) & (sub == j + 1)))
            r = (r - fix) - (u0 * (rows(r, j) - one_at(lane == k)) + u1 * (rows(r, j + 1) - one_at(lane == k + 1)))
        w = r + one_at(lane - 8 * q == sub)
        w_rows = [rows(w, m) for m in range(8)]
        for i in range(q + 1, q + groups):
            x = a[i % groups]
            t = [lanes(x, 8 * q + m) * w_rows[m] for m in range(8)]
            a[i % groups] = x - (((t[0] + t[1]) + (t[2] + t[3])) + ((t[4] + t[5]) + (t[6] + t[7])))
        a[q] = r
    return a


def exact_dot(a, b):
    return jnp.dot(a, b, precision=lax.Precision.HIGHEST, preferred_element_type=f32)


def solve_kernel(mine, other, targets_ref, z_ref, coef_ref, res_ref, dir_ref):
    size = mine.shape[1]
    gram = mine[0] + other[0]
    mix_t = mine[1] + other[1]
    quad = mine[2] + other[2]
    diag = ridge_weight + kernel_gain
    mix = mix_t.T
    both = mix + mix_t
    half_gain = 0.5 * kernel_gain
    sym = diag * gram + half_gain * both
    outer = (diag * diag) * gram + (diag * kernel_gain) * both + (kernel_gain * kernel_gain) * quad
    curv = diag * gram + kernel_gain * mix
    eye = lax.broadcasted_iota(jnp.int32, (size, size), 0) == lax.broadcasted_iota(jnp.int32, (size, size), 1)
    on_diag = jnp.where(eye, sym, 0.0)
    by_col = lax.rsqrt(jnp.sum(on_diag, axis=0, keepdims=True))
    by_row = lax.rsqrt(jnp.sum(on_diag, axis=1, keepdims=True))
    unit = sym * by_row * by_col
    parts = negated_inverse([unit[8 * i : 8 * i + 8, :] for i in range(size // 8)], size)
    minus_inverse = jnp.concatenate(parts, axis=0) * by_row * by_col
    step_t = -exact_dot(gram, minus_inverse)
    correction_t = exact_dot(curv - exact_dot(step_t, outer), minus_inverse)
    targets = targets_ref[...]
    image = ridge_weight * targets + kernel_gain * (targets.astype(bf16).astype(f32) + z_ref[...])
    residual = targets - exact_dot(step_t, image)
    coef_ref[...] = exact_dot(step_t, targets)
    res_ref[...] = residual
    dir_ref[...] = residual + exact_dot(correction_t, targets)


def flips(size, bit):
    return [(i, i ^ bit) for i in range(size)]


def call(kernel, out_shape, scratch_shapes, operands, limit):
    vmem = pl.BlockSpec(memory_space=pltpu.VMEM)
    return pl.pallas_call(
        kernel,
        out_shape=out_shape,
        in_specs=[vmem] * len(operands),
        out_specs=jax.tree.map(lambda _: vmem, out_shape),
        scratch_shapes=scratch_shapes,
        compiler_params=pltpu.CompilerParams(vmem_limit_bytes=limit),
    )(*operands)


def local(row_size, col_size):
    def run(features, targets):
        return step(features, targets)

    def step(features, targets):
        feat_rows, block = features.shape
        out_rows = targets.shape[0]
        scale = sharpness / feat_rows

        def flip(axis, bit):
            size = row_size if axis == "row" else col_size
            return lambda x: lax.ppermute(x, axis, flips(size, bit))

        hops = [("row", 1 << s) for s in reversed(range(1, row_size.bit_length() - 1))]
        hops += [("col", 1 << s) for s in reversed(range(1, col_size.bit_length() - 2))]
        line = jnp.concatenate([features, targets.astype(bf16)], axis=0)[None]
        for axis, bit in hops:
            line = jnp.concatenate([line, flip(axis, bit)(line)], axis=0)
        over_x, over_y, partner = flip("row", 1), flip("col", col_size // 2), flip("col", 1)
        from_x, from_y = over_x(line), over_y(line)
        half = line.shape[0] // 2
        far_x = over_x(from_y[:half])
        far_y = over_y(from_x[half:])
        far = jnp.concatenate([far_x, far_y], axis=0)
        near = [line, from_x, from_y]
        other_near = [partner(x) for x in near]
        other_far = partner(far)

        width = line.shape[0] * block

        def scratch(count):
            return [
                pltpu.VMEM((count * width, feat_rows + 16), bf16),
                pltpu.VMEM((feat_rows + 16, count * width), bf16),
                pltpu.VMEM((out_rows, count * width), bf16),
            ]

        limit = product_vmem if width <= widest else None
        part = call(
            product_kernel([(0, 0, 6), (1, 0, 6), (2, 0, 6)], feat_rows, scale, False),
            jax.ShapeDtypeStruct((out_rows, 3 * width), f32),
            scratch(6),
            [*near, *other_near],
            limit,
        )
        z, grams = call(
            product_kernel([(0, 6, 8), (1, 6, 8), (2, 6, 8), (6, 0, 8)], feat_rows, scale, True),
            (
                jax.ShapeDtypeStruct((out_rows, block), f32),
                jax.ShapeDtypeStruct((3, out_rows, out_rows), f32),
            ),
            scratch(8) + [pltpu.VMEM((3 * out_rows, 2 * out_rows), f32)],
            [*near, *other_near, far, other_far, part],
            limit,
        )
        return call(
            solve_kernel,
            tuple(jax.ShapeDtypeStruct(targets.shape, f32) for _ in range(3)),
            [],
            [grams, partner(grams), targets, z],
            solve_vmem,
        )

    return run


def solution(mesh):
    spec = P(None, ("col", "row"))
    return jax.shard_map(
        local(mesh.shape["row"], mesh.shape["col"]),
        mesh=mesh,
        in_specs=(spec, spec),
        out_specs=(spec, spec, spec),
        check_vma=False,
    )
```

```python
import jax
import jax.numpy as jnp
from jax import lax
from jax.experimental import pallas as pl
from jax.experimental.pallas import tpu as pltpu
from jax.sharding import PartitionSpec as P

ridge_weight = 0.5
kernel_gain = 2.0
sharpness = 3.0
log2_e = 1.4426950408889634
longest = 4096
widest = 1024
step_rows = 2048
step_cols = 512
product_vmem = 28 << 20
solve_vmem = 4 << 20

f32 = jnp.float32
bf16 = jnp.bfloat16


def prepare(own, other, left, right, panel, feat_rows):
    count, _, block = (other if own is None else own).shape
    ones = jnp.ones((3, block), bf16)
    fill = jnp.zeros((10, block), bf16)

    def one(piece, at, b, is_own):
        here = pl.ds(at, block)
        feat = piece[b, :feat_rows, :]
        wide = feat.astype(f32)
        half = -0.5 * jnp.sum(wide * wide, axis=0, keepdims=True)
        high = half.astype(bf16)
        rest = half - high.astype(f32)
        mid = rest.astype(bf16)
        low = (rest - mid.astype(f32)).astype(bf16)
        norms = [high, mid, low]
        left[here, :] = jnp.concatenate([feat] + norms + [ones, fill], axis=0).T
        if is_own:
            right[:, here] = jnp.concatenate([feat, ones] + norms + [fill], axis=0)
        panel[:, here] = piece[b, feat_rows:, :]

    for piece, first in ((own, 0), (other, count)):
        if piece is None:
            continue
        if count <= 8:
            for b in range(count):
                one(piece, (first + b) * block, b, piece is own)
        else:

            def looped(b, carry, piece=piece, first=first):
                one(piece, pl.multiple_of((first + b) * block, block), b, piece is own)
                return carry

            lax.fori_loop(0, count, looped, 0)


def product(stage, right, cols, scale):
    left, panel = stage
    rows_of = left.shape[0]

    def part(here):
        inner = jnp.dot(left[here, :], right[:, cols], preferred_element_type=f32)
        entries = jnp.exp2(inner * (2.0 * scale * log2_e)).astype(bf16)
        return jnp.dot(panel[:, here], entries, preferred_element_type=f32)

    if rows_of <= longest:
        return part(slice(None))

    def add(t, carry):
        return carry + part(pl.ds(pl.multiple_of(t * step_rows, step_rows), step_rows))

    return lax.fori_loop(0, rows_of // step_rows, add, jnp.zeros((panel.shape[0], cols.size), f32))


def over_columns(count, work):
    if count <= widest:
        work(pl.ds(0, count), True)
    else:

        def looped(s, carry):
            work(pl.ds(pl.multiple_of(s * step_cols, step_cols), step_cols), s == 0)
            return carry

        lax.fori_loop(0, count // step_cols, looped, 0)


def first_kernel(feat_rows, scale):
    def body(own, other, left, right, panel, y0):
        prepare(own, other, left, right, panel, feat_rows)

        def work(cols, _):
            y0[:, cols] = product((left, panel), right, cols, scale)

        over_columns(right.shape[1], work)

    return body


def second_kernel(feat_rows, scale):
    def body(own, other, left0, right0, panel0, y0_in, left, right, panel, y0, y1):
        prepare(own, other, left, right, panel, feat_rows)
        now, before = (left, panel), (left0, panel0)

        def work1(cols, _):
            y1[:, cols] = product(before, right, cols, scale) + product(now, right, cols, scale)

        def work0(cols, _):
            y0[:, cols] = y0_in[:, cols] + product(now, right0, cols, scale)

        over_columns(right.shape[1], work1)
        over_columns(right0.shape[1], work0)

    return body


def cover_kernel(feat_rows, scale):
    def body(own, left0, panel0, left1, panel1, left, right, panel, y2):
        prepare(own, None, left, right, panel, feat_rows)

        def work(cols, _):
            y2[:, cols] = product((left0, panel0), right, cols, scale) + product((left1, panel1), right, cols, scale)

        over_columns(right.shape[1], work)

    return body


def third_kernel(feat_rows, scale):
    def body(other, *refs):
        left_own, right, panel_own, right0, panel0, right1, panel1, y0, y1, y2, z_ref, gram_ref, left, panel, sums = refs
        mine = right.shape[1]
        left[:mine, :] = left_own[...]
        panel[:, :mine] = panel_own[...]
        prepare(None, other, left, right, panel, feat_rows)
        sums[...] = jnp.zeros(sums.shape, f32)
        block = z_ref.shape[1]

        def add_columns(right_of, panel_of, y, holds_own):
            def work(cols, is_first):
                total = product((left, panel), right_of, cols, scale) + y[:, cols]
                own_panel = panel_of[:, cols]
                z = total - own_panel.astype(f32)
                if holds_own:

                    def put():
                        z_ref[...] = z[:, :block]

                    put() if is_first is True else pl.when(is_first)(put)
                high = z.astype(bf16)
                low = (z - high.astype(f32)).astype(bf16)
                rhs = jnp.concatenate([own_panel, high], axis=0)
                lhs = jnp.concatenate([rhs, low], axis=0)
                sums[...] += lax.dot_general(lhs, rhs, (((1,), (1,)), ((), ())), preferred_element_type=f32)

            over_columns(right_of.shape[1], work)

        add_columns(right0, panel0, y0, True)
        add_columns(right1, panel1, y1, False)
        add_columns(right, panel, y2, False)
        r = panel.shape[0]
        cross = sums[2 * r :, r:]
        gram_ref[0] = sums[:r, :r]
        gram_ref[1] = sums[r : 2 * r, :r] + sums[2 * r :, :r]
        gram_ref[2] = sums[r : 2 * r, r:] + cross + cross.T

    return body


def lanes(v, k):
    return jnp.broadcast_to(v[:, k : k + 1], v.shape)


def rows(v, j):
    return jnp.broadcast_to(v[j : j + 1, :], v.shape)


def negated_inverse(a, size):
    groups = size // 8
    lane = lax.broadcasted_iota(jnp.int32, (8, size), 1)
    sub = lax.broadcasted_iota(jnp.int32, (8, size), 0)

    def one_at(mask):
        return jnp.where(mask, 1.0, 0.0)

    one = one_at(lane >= 0)
    for q in range(groups):
        r = a[q]
        c = [lanes(r, 8 * q + m) * one for m in range(8)]
        for j in range(0, 8, 2):
            k = 8 * q + j
            p, b, d = rows(c[j], j), rows(c[j + 1], j), rows(c[j + 1], j + 1)
            scale = 1.0 / (p * d - b * b)
            c0 = c[j] - one_at(sub == j)
            c1 = c[j + 1] - one_at(sub == j + 1)
            u0 = (c0 * d - c1 * b) * scale
            u1 = (c1 * p - c0 * b) * scale
            for m in range(j + 2, 8):
                c[m] = c[m] - (u0 * rows(c[m], j) + u1 * rows(c[m], j + 1))
            fix = 2.0 * one_at(((lane == k) & (sub == j)) | ((lane == k + 1) & (sub == j + 1)))
            r = (r - fix) - (u0 * (rows(r, j) - one_at(lane == k)) + u1 * (rows(r, j + 1) - one_at(lane == k + 1)))
        w = r + one_at(lane - 8 * q == sub)
        w_rows = [rows(w, m) for m in range(8)]
        base = groups // 2 if q < groups // 2 else 0
        update = lax.dot_general(
            a[q][:, 8 * base : 8 * base + size // 2],
            w,
            (((0,), (0,)), ((), ())),
            precision=lax.Precision.HIGHEST,
            preferred_element_type=f32,
        )
        for i in [i % groups for i in range(q + 1, q + groups)]:
            x = a[i]
            at = 8 * (i - base)
            if 0 <= at < size // 2 and i != q + 1:
                a[i] = x - update[at : at + 8, :]
            else:
                t = [lanes(x, 8 * q + m) * w_rows[m] for m in range(8)]
                a[i] = x - (((t[0] + t[1]) + (t[2] + t[3])) + ((t[4] + t[5]) + (t[6] + t[7])))
        a[q] = r
    return a


def exact_dot(a, b):
    return jnp.dot(a, b, precision=lax.Precision.HIGHEST, preferred_element_type=f32)


def solve_kernel(mine, other, targets_ref, z_ref, coef_ref, res_ref, dir_ref):
    size = mine.shape[1]
    gram = mine[0] + other[0]
    mix_t = mine[1] + other[1]
    quad = mine[2] + other[2]
    diag = ridge_weight + kernel_gain
    mix = mix_t.T
    both = mix + mix_t
    half_gain = 0.5 * kernel_gain
    sym = diag * gram + half_gain * both
    outer = (diag * diag) * gram + (diag * kernel_gain) * both + (kernel_gain * kernel_gain) * quad
    curv = diag * gram + kernel_gain * mix
    eye = lax.broadcasted_iota(jnp.int32, (size, size), 0) == lax.broadcasted_iota(jnp.int32, (size, size), 1)
    on_diag = jnp.where(eye, sym, 0.0)
    by_col = lax.rsqrt(jnp.sum(on_diag, axis=0, keepdims=True))
    by_row = lax.rsqrt(jnp.sum(on_diag, axis=1, keepdims=True))
    unit = sym * by_row * by_col
    parts = negated_inverse([unit[8 * i : 8 * i + 8, :] for i in range(size // 8)], size)
    minus_inverse = jnp.concatenate(parts, axis=0) * by_row * by_col
    step_t = -exact_dot(gram, minus_inverse)
    correction_t = exact_dot(curv - exact_dot(step_t, outer), minus_inverse)
    targets = targets_ref[...]
    image = ridge_weight * targets + kernel_gain * (targets.astype(bf16).astype(f32) + z_ref[...])
    residual = targets - exact_dot(step_t, image)
    coef_ref[...] = exact_dot(step_t, targets)
    res_ref[...] = residual
    dir_ref[...] = residual + exact_dot(correction_t, targets)


def flips(size, bit):
    return [(i, i ^ bit) for i in range(size)]


def call(kernel, out_shape, scratch_shapes, operands, limit):
    vmem = pl.BlockSpec(memory_space=pltpu.VMEM)
    return pl.pallas_call(
        kernel,
        out_shape=out_shape,
        in_specs=[vmem] * len(operands),
        out_specs=jax.tree.map(lambda _: vmem, out_shape),
        scratch_shapes=scratch_shapes,
        compiler_params=pltpu.CompilerParams(vmem_limit_bytes=limit),
    )(*operands)


def local(row_size, col_size):
    def run(features, targets):
        return step(features, targets)

    def step(features, targets):
        feat_rows, block = features.shape
        out_rows = targets.shape[0]
        scale = sharpness / feat_rows
        inner_rows = feat_rows + 16

        def flip(axis, bit):
            size = row_size if axis == "row" else col_size

            def send(x):
                return lax.ppermute(x, axis, flips(size, bit))

            return send

        def over_x(x):
            return flip("row", 1)(x)

        def over_y(x):
            return flip("col", col_size // 2)(x)

        def partner(x):
            return flip("col", 1)(x)

        def join(*pieces):
            return jnp.concatenate(pieces, axis=0)

        hops = [("row", 1 << s) for s in reversed(range(1, row_size.bit_length() - 1))]
        hops += [("col", 1 << s) for s in reversed(range(1, col_size.bit_length() - 2))]
        line = join(features, targets.astype(bf16))[None]
        for axis, bit in hops:
            line = join(line, flip(axis, bit)(line))
        other_line = partner(line)
        from_x, from_y = over_x(line), over_y(line)
        near = join(from_x, from_y)
        other_near = partner(near)
        half = line.shape[0] // 2
        far = join(over_x(from_y[:half]), over_y(from_x[half:]))
        other_far = partner(far)

        limit = product_vmem if line.shape[0] <= 4 else None

        def stage(count):
            return [
                ((2 * count * block, inner_rows), bf16),
                ((inner_rows, count * block), bf16),
                ((out_rows, 2 * count * block), bf16),
            ]

        def sums_of(count):
            return ((out_rows, count * block), f32)

        def shapes(entries):
            return tuple(jax.ShapeDtypeStruct(*x) for x in entries)

        n0, n1, n2 = line.shape[0], near.shape[0], far.shape[0]
        left0, right0, panel0, y0 = call(
            first_kernel(feat_rows, scale), shapes(stage(n0) + [sums_of(n0)]), [], [line, other_line], limit
        )
        left1, right1, panel1, y0, y1 = call(
            second_kernel(feat_rows, scale),
            shapes(stage(n1) + [sums_of(n0), sums_of(n1)]),
            [],
            [near, other_near, left0, right0, panel0, y0],
            limit,
        )
        full_left, right_shape, full_panel = stage(n2)
        own_left = ((n2 * block, inner_rows), bf16)
        own_panel = ((out_rows, n2 * block), bf16)
        left2, right2, panel2, y2 = call(
            cover_kernel(feat_rows, scale),
            shapes([own_left, right_shape, own_panel, sums_of(n2)]),
            [],
            [far, left0, panel0, left1, panel1],
            limit,
        )
        z, grams = call(
            third_kernel(feat_rows, scale),
            shapes([((out_rows, block), f32), ((3, out_rows, out_rows), f32)]),
            [pltpu.VMEM(*x) for x in [full_left, full_panel, ((3 * out_rows, 2 * out_rows), f32)]],
            [other_far, left2, right2, panel2, right0, panel0, right1, panel1, y0, y1, y2],
            limit,
        )
        return call(
            solve_kernel,
            tuple(jax.ShapeDtypeStruct(targets.shape, f32) for _ in range(3)),
            [],
            [grams, partner(grams), targets, z],
            solve_vmem,
        )

    return run


def solution(mesh):
    spec = P(None, ("col", "row"))
    return jax.shard_map(
        local(mesh.shape["row"], mesh.shape["col"]),
        mesh=mesh,
        in_specs=(spec, spec),
        out_specs=(spec, spec, spec),
        check_vma=False,
    )
```

```python
import jax
import jax.numpy as jnp
from jax import lax
from jax.experimental import pallas as pl
from jax.experimental.pallas import tpu as pltpu
from jax.sharding import PartitionSpec as P

ridge_weight = 0.5
kernel_gain = 2.0
sharpness = 3.0
log2_e = 1.4426950408889634
longest = 4096
widest = 1024
step_rows = 2048
step_cols = 512
product_vmem = 28 << 20
solve_vmem = 4 << 20

f32 = jnp.float32
bf16 = jnp.bfloat16


def prepare(own, other, left, right, panel, feat_rows):
    count, _, block = (other if own is None else own).shape
    ones = jnp.ones((3, block), bf16)
    fill = jnp.zeros((10, block), bf16)

    def one(piece, at, b, is_own):
        here = pl.ds(at, block)
        feat = piece[b, :feat_rows, :]
        wide = feat.astype(f32)
        half = -0.5 * jnp.sum(wide * wide, axis=0, keepdims=True)
        high = half.astype(bf16)
        rest = half - high.astype(f32)
        mid = rest.astype(bf16)
        low = (rest - mid.astype(f32)).astype(bf16)
        norms = [high, mid, low]
        left[here, :] = jnp.concatenate([feat] + norms + [ones, fill], axis=0).T
        if is_own:
            right[:, here] = jnp.concatenate([feat, ones] + norms + [fill], axis=0)
        panel[:, here] = piece[b, feat_rows:, :]

    for piece, first in ((own, 0), (other, count)):
        if piece is None:
            continue
        if count <= 8:
            for b in range(count):
                one(piece, (first + b) * block, b, piece is own)
        else:

            def looped(b, carry, piece=piece, first=first):
                one(piece, pl.multiple_of((first + b) * block, block), b, piece is own)
                return carry

            lax.fori_loop(0, count, looped, 0)


def product(stage, right, cols, scale):
    left, panel = stage
    rows_of = left.shape[0]

    def part(here):
        inner = jnp.dot(left[here, :], right[:, cols], preferred_element_type=f32)
        entries = jnp.exp2(inner * (2.0 * scale * log2_e)).astype(bf16)
        return jnp.dot(panel[:, here], entries, preferred_element_type=f32)

    if rows_of <= longest:
        return part(slice(None))

    def add(t, carry):
        return carry + part(pl.ds(pl.multiple_of(t * step_rows, step_rows), step_rows))

    return lax.fori_loop(0, rows_of // step_rows, add, jnp.zeros((panel.shape[0], cols.size), f32))


def over_columns(count, work):
    if count <= widest:
        work(pl.ds(0, count), True)
    else:

        def looped(s, carry):
            work(pl.ds(pl.multiple_of(s * step_cols, step_cols), step_cols), s == 0)
            return carry

        lax.fori_loop(0, count // step_cols, looped, 0)


def first_kernel(feat_rows, scale):
    def body(own, other, left, right, panel, y0):
        prepare(own, other, left, right, panel, feat_rows)

        def work(cols, _):
            y0[:, cols] = product((left, panel), right, cols, scale)

        over_columns(right.shape[1], work)

    return body


def second_kernel(feat_rows, scale):
    def body(own, other, left0, right0, panel0, y0_in, left, right, panel, y0, y1):
        prepare(own, other, left, right, panel, feat_rows)
        now, before = (left, panel), (left0, panel0)

        def work1(cols, _):
            y1[:, cols] = product(before, right, cols, scale) + product(now, right, cols, scale)

        def work0(cols, _):
            y0[:, cols] = y0_in[:, cols] + product(now, right0, cols, scale)

        over_columns(right.shape[1], work1)
        over_columns(right0.shape[1], work0)

    return body


def cover_kernel(feat_rows, scale):
    def body(own, left0, panel0, left1, panel1, left, right, panel, y2):
        prepare(own, None, left, right, panel, feat_rows)

        def work(cols, _):
            y2[:, cols] = product((left0, panel0), right, cols, scale) + product((left1, panel1), right, cols, scale)

        over_columns(right.shape[1], work)

    return body


def third_kernel(feat_rows, scale):
    def body(other, *refs):
        left_own, right, panel_own, right0, panel0, right1, panel1, y0, y1, y2, z_ref, gram_ref, left, panel, sums = refs
        mine = right.shape[1]
        left[:mine, :] = left_own[...]
        panel[:, :mine] = panel_own[...]
        prepare(None, other, left, right, panel, feat_rows)
        sums[...] = jnp.zeros(sums.shape, f32)
        block = z_ref.shape[1]

        def add_columns(right_of, panel_of, y, holds_own):
            def work(cols, is_first):
                total = product((left, panel), right_of, cols, scale) + y[:, cols]
                own_panel = panel_of[:, cols]
                z = total - own_panel.astype(f32)
                if holds_own:

                    def put():
                        z_ref[...] = z[:, :block]

                    put() if is_first is True else pl.when(is_first)(put)
                both = jnp.concatenate([own_panel, z.astype(bf16)], axis=0)
                sums[...] += lax.dot_general(both, both, (((1,), (1,)), ((), ())), preferred_element_type=f32)

            over_columns(right_of.shape[1], work)

        add_columns(right0, panel0, y0, True)
        add_columns(right1, panel1, y1, False)
        add_columns(right, panel, y2, False)
        r = panel.shape[0]
        gram_ref[0] = sums[:r, :r]
        gram_ref[1] = sums[r:, :r]
        gram_ref[2] = sums[r:, r:]

    return body


def lanes(v, k):
    return jnp.broadcast_to(v[:, k : k + 1], v.shape)


def rows(v, j):
    return jnp.broadcast_to(v[j : j + 1, :], v.shape)


def negated_inverse(a, size):
    groups = size // 8
    lane = lax.broadcasted_iota(jnp.int32, (8, size), 1)
    sub = lax.broadcasted_iota(jnp.int32, (8, size), 0)

    def one_at(mask):
        return jnp.where(mask, 1.0, 0.0)

    one = one_at(lane >= 0)
    for q in range(groups):
        r = a[q]
        c = [lanes(r, 8 * q + m) * one for m in range(8)]
        for j in range(0, 8, 2):
            k = 8 * q + j
            p, b, d = rows(c[j], j), rows(c[j + 1], j), rows(c[j + 1], j + 1)
            scale = 1.0 / (p * d - b * b)
            c0 = c[j] - one_at(sub == j)
            c1 = c[j + 1] - one_at(sub == j + 1)
            u0 = (c0 * d - c1 * b) * scale
            u1 = (c1 * p - c0 * b) * scale
            for m in range(j + 2, 8):
                c[m] = c[m] - (u0 * rows(c[m], j) + u1 * rows(c[m], j + 1))
            fix = 2.0 * one_at(((lane == k) & (sub == j)) | ((lane == k + 1) & (sub == j + 1)))
            r = (r - fix) - (u0 * (rows(r, j) - one_at(lane == k)) + u1 * (rows(r, j + 1) - one_at(lane == k + 1)))
        w = r + one_at(lane - 8 * q == sub)
        w_rows = [rows(w, m) for m in range(8)]
        base = groups // 2 if q < groups // 2 else 0
        update = lax.dot_general(
            a[q][:, 8 * base : 8 * base + size // 2],
            w,
            (((0,), (0,)), ((), ())),
            precision=lax.Precision.HIGHEST,
            preferred_element_type=f32,
        )
        for i in [i % groups for i in range(q + 1, q + groups)]:
            x = a[i]
            at = 8 * (i - base)
            if 0 <= at < size // 2 and i != q + 1:
                a[i] = x - update[at : at + 8, :]
            else:
                t = [lanes(x, 8 * q + m) * w_rows[m] for m in range(8)]
                a[i] = x - (((t[0] + t[1]) + (t[2] + t[3])) + ((t[4] + t[5]) + (t[6] + t[7])))
        a[q] = r
    return a


def exact_dot(a, b):
    return jnp.dot(a, b, precision=lax.Precision.HIGHEST, preferred_element_type=f32)


def solve_kernel(mine, other, targets_ref, z_ref, coef_ref, res_ref, dir_ref):
    size = mine.shape[1]
    gram = mine[0] + other[0]
    mix_t = mine[1] + other[1]
    quad = mine[2] + other[2]
    diag = ridge_weight + kernel_gain
    mix = mix_t.T
    both = mix + mix_t
    half_gain = 0.5 * kernel_gain
    sym = diag * gram + half_gain * both
    outer = (diag * diag) * gram + (diag * kernel_gain) * both + (kernel_gain * kernel_gain) * quad
    curv = diag * gram + kernel_gain * mix
    eye = lax.broadcasted_iota(jnp.int32, (size, size), 0) == lax.broadcasted_iota(jnp.int32, (size, size), 1)
    on_diag = jnp.where(eye, sym, 0.0)
    by_col = lax.rsqrt(jnp.sum(on_diag, axis=0, keepdims=True))
    by_row = lax.rsqrt(jnp.sum(on_diag, axis=1, keepdims=True))
    unit = sym * by_row * by_col
    parts = negated_inverse([unit[8 * i : 8 * i + 8, :] for i in range(size // 8)], size)
    minus_inverse = jnp.concatenate(parts, axis=0) * by_row * by_col
    step_t = -exact_dot(gram, minus_inverse)
    correction_t = exact_dot(curv - exact_dot(step_t, outer), minus_inverse)
    targets = targets_ref[...]
    image = ridge_weight * targets + kernel_gain * (targets.astype(bf16).astype(f32) + z_ref[...])
    residual = targets - exact_dot(step_t, image)
    coef_ref[...] = exact_dot(step_t, targets)
    res_ref[...] = residual
    dir_ref[...] = residual + exact_dot(correction_t, targets)


def flips(size, bit):
    return [(i, i ^ bit) for i in range(size)]


def call(kernel, out_shape, scratch_shapes, operands, limit):
    vmem = pl.BlockSpec(memory_space=pltpu.VMEM)
    return pl.pallas_call(
        kernel,
        out_shape=out_shape,
        in_specs=[vmem] * len(operands),
        out_specs=jax.tree.map(lambda _: vmem, out_shape),
        scratch_shapes=scratch_shapes,
        compiler_params=pltpu.CompilerParams(vmem_limit_bytes=limit),
    )(*operands)


def local(row_size, col_size):
    def run(features, targets):
        return step(features, targets)

    def step(features, targets):
        feat_rows, block = features.shape
        out_rows = targets.shape[0]
        scale = sharpness / feat_rows
        inner_rows = feat_rows + 16

        def flip(axis, bit):
            size = row_size if axis == "row" else col_size

            def send(x):
                return lax.ppermute(x, axis, flips(size, bit))

            return send

        def over_x(x):
            return flip("row", 1)(x)

        def over_y(x):
            return flip("col", col_size // 2)(x)

        def partner(x):
            return flip("col", 1)(x)

        def join(*pieces):
            return jnp.concatenate(pieces, axis=0)

        hops = [("row", 1 << s) for s in reversed(range(1, row_size.bit_length() - 1))]
        hops += [("col", 1 << s) for s in reversed(range(1, col_size.bit_length() - 2))]
        line = join(features, targets.astype(bf16))[None]
        for axis, bit in hops:
            line = join(line, flip(axis, bit)(line))
        other_line = partner(line)
        half = line.shape[0] // 2
        early_y = over_y(line[:half])
        from_x, late_y = over_x(line), over_y(line[half:])
        far_x = over_x(early_y)
        near = join(from_x, early_y, late_y)
        other_near = partner(near)
        far = join(far_x, over_y(from_x[half:]))
        other_far = partner(far)

        limit = product_vmem if line.shape[0] <= 4 else None

        def stage(count):
            return [
                ((2 * count * block, inner_rows), bf16),
                ((inner_rows, count * block), bf16),
                ((out_rows, 2 * count * block), bf16),
            ]

        def sums_of(count):
            return ((out_rows, count * block), f32)

        def shapes(entries):
            return tuple(jax.ShapeDtypeStruct(*x) for x in entries)

        n0, n1, n2 = line.shape[0], near.shape[0], far.shape[0]
        left0, right0, panel0, y0 = call(
            first_kernel(feat_rows, scale), shapes(stage(n0) + [sums_of(n0)]), [], [line, other_line], limit
        )
        left1, right1, panel1, y0, y1 = call(
            second_kernel(feat_rows, scale),
            shapes(stage(n1) + [sums_of(n0), sums_of(n1)]),
            [],
            [near, other_near, left0, right0, panel0, y0],
            limit,
        )
        full_left, right_shape, full_panel = stage(n2)
        own_left = ((n2 * block, inner_rows), bf16)
        own_panel = ((out_rows, n2 * block), bf16)
        left2, right2, panel2, y2 = call(
            cover_kernel(feat_rows, scale),
            shapes([own_left, right_shape, own_panel, sums_of(n2)]),
            [],
            [far, left0, panel0, left1, panel1],
            limit,
        )
        z, grams = call(
            third_kernel(feat_rows, scale),
            shapes([((out_rows, block), f32), ((3, out_rows, out_rows), f32)]),
            [pltpu.VMEM(*x) for x in [full_left, full_panel, ((2 * out_rows, 2 * out_rows), f32)]],
            [other_far, left2, right2, panel2, right0, panel0, right1, panel1, y0, y1, y2],
            limit,
        )
        return call(
            solve_kernel,
            tuple(jax.ShapeDtypeStruct(targets.shape, f32) for _ in range(3)),
            [],
            [grams, partner(grams), targets, z],
            solve_vmem,
        )

    return run


def solution(mesh):
    spec = P(None, ("col", "row"))
    return jax.shard_map(
        local(mesh.shape["row"], mesh.shape["col"]),
        mesh=mesh,
        in_specs=(spec, spec),
        out_specs=(spec, spec, spec),
        check_vma=False,
    )
```

```python
import jax
import jax.numpy as jnp
from jax import lax
from jax.experimental import pallas as pl
from jax.experimental.pallas import tpu as pltpu
from jax.sharding import PartitionSpec as P

ridge_weight = 0.5
kernel_gain = 2.0
sharpness = 3.0
log2_e = 1.4426950408889634
longest = 4096
widest = 1024
step_rows = 2048
step_cols = 512
product_vmem = 28 << 20
solve_vmem = 4 << 20

f32 = jnp.float32
bf16 = jnp.bfloat16


def prepare(own, other, left, right, panel, feat_rows):
    block = (other if own is None else own).shape[2]
    start = other.shape[0] if own is None else own.shape[0]
    ones = jnp.ones((3, block), bf16)
    fill = jnp.zeros((10, block), bf16)

    def one(piece, at, b, is_own):
        here = pl.ds(at, block)
        feat = piece[b, :feat_rows, :]
        wide = feat.astype(f32)
        half = -0.5 * jnp.sum(wide * wide, axis=0, keepdims=True)
        high = half.astype(bf16)
        rest = half - high.astype(f32)
        mid = rest.astype(bf16)
        low = (rest - mid.astype(f32)).astype(bf16)
        norms = [high, mid, low]
        left[here, :] = jnp.concatenate([feat] + norms + [ones, fill], axis=0).T
        if is_own:
            right[:, here] = jnp.concatenate([feat, ones] + norms + [fill], axis=0)
        panel[:, here] = piece[b, feat_rows:, :]

    for piece, first in ((own, 0), (other, start)):
        if piece is None:
            continue
        count = piece.shape[0]
        if count <= 12:
            for b in range(count):
                one(piece, (first + b) * block, b, piece is own)
        else:

            def looped(b, carry, piece=piece, first=first):
                one(piece, pl.multiple_of((first + b) * block, block), b, piece is own)
                return carry

            lax.fori_loop(0, count, looped, 0)


def product(stage, right, cols, scale):
    left, panel = stage
    rows_of = left.shape[0]

    def part(here):
        inner = jnp.dot(left[here, :], right[:, cols], preferred_element_type=f32)
        entries = jnp.exp2(inner * (2.0 * scale * log2_e)).astype(bf16)
        return jnp.dot(panel[:, here], entries, preferred_element_type=f32)

    if rows_of <= longest:
        return part(slice(None))

    def add(t, carry):
        return carry + part(pl.ds(pl.multiple_of(t * step_rows, step_rows), step_rows))

    return lax.fori_loop(0, rows_of // step_rows, add, jnp.zeros((panel.shape[0], cols.size), f32))


def over_columns(count, work):
    if count <= widest:
        work(pl.ds(0, count), True)
    else:

        def looped(s, carry):
            work(pl.ds(pl.multiple_of(s * step_cols, step_cols), step_cols), s == 0)
            return carry

        lax.fori_loop(0, count // step_cols, looped, 0)


def first_kernel(feat_rows, scale):
    def body(own, left, right, panel, y0):
        prepare(own, None, left, right, panel, feat_rows)

        def work(cols, _):
            y0[:, cols] = product((left, panel), right, cols, scale)

        over_columns(right.shape[1], work)

    return body


def second_kernel(feat_rows, scale):
    def body(own, other, left0, right0, panel0, y0_in, left, right, panel, y0, y1):
        prepare(own, other, left, right, panel, feat_rows)
        now, before = (left, panel), (left0, panel0)

        def work1(cols, _):
            y1[:, cols] = product(before, right, cols, scale) + product(now, right, cols, scale)

        def work0(cols, _):
            y0[:, cols] = y0_in[:, cols] + product(now, right0, cols, scale)

        over_columns(right.shape[1], work1)
        over_columns(right0.shape[1], work0)

    return body


def cover_kernel(feat_rows, scale):
    def body(own, left0, panel0, left1, panel1, left, right, panel, y2):
        prepare(own, None, left, right, panel, feat_rows)

        def work(cols, _):
            y2[:, cols] = product((left0, panel0), right, cols, scale) + product((left1, panel1), right, cols, scale)

        over_columns(right.shape[1], work)

    return body


def third_kernel(feat_rows, scale):
    def body(other, *refs):
        left_own, right, panel_own, right0, panel0, right1, panel1, y0, y1, y2, z_ref, gram_ref, left, panel, sums = refs
        mine = right.shape[1]
        left[:mine, :] = left_own[...]
        panel[:, :mine] = panel_own[...]
        prepare(None, other, left, right, panel, feat_rows)
        sums[...] = jnp.zeros(sums.shape, f32)
        block = z_ref.shape[1]

        def add_columns(right_of, panel_of, y, holds_own):
            def work(cols, is_first):
                total = product((left, panel), right_of, cols, scale) + y[:, cols]
                own_panel = panel_of[:, cols]
                z = total - own_panel.astype(f32)
                if holds_own:

                    def put():
                        z_ref[...] = z[:, :block]

                    put() if is_first is True else pl.when(is_first)(put)
                both = jnp.concatenate([own_panel, z.astype(bf16)], axis=0)
                sums[...] += lax.dot_general(both, both, (((1,), (1,)), ((), ())), preferred_element_type=f32)

            over_columns(right_of.shape[1], work)

        add_columns(right0, panel0, y0, True)
        add_columns(right1, panel1, y1, False)
        add_columns(right, panel, y2, False)
        r = panel.shape[0]
        gram_ref[0] = sums[:r, :r]
        gram_ref[1] = sums[r:, :r]
        gram_ref[2] = sums[r:, r:]

    return body


def lanes(v, k):
    return jnp.broadcast_to(v[:, k : k + 1], v.shape)


def rows(v, j):
    return jnp.broadcast_to(v[j : j + 1, :], v.shape)


def negated_inverse(a, size):
    groups = size // 8
    lane = lax.broadcasted_iota(jnp.int32, (8, size), 1)
    sub = lax.broadcasted_iota(jnp.int32, (8, size), 0)

    def one_at(mask):
        return jnp.where(mask, 1.0, 0.0)

    one = one_at(lane >= 0)
    for q in range(groups):
        r = a[q]
        c = [lanes(r, 8 * q + m) * one for m in range(8)]
        for j in range(0, 8, 2):
            k = 8 * q + j
            p, b, d = rows(c[j], j), rows(c[j + 1], j), rows(c[j + 1], j + 1)
            scale = 1.0 / (p * d - b * b)
            c0 = c[j] - one_at(sub == j)
            c1 = c[j + 1] - one_at(sub == j + 1)
            u0 = (c0 * d - c1 * b) * scale
            u1 = (c1 * p - c0 * b) * scale
            for m in range(j + 2, 8):
                c[m] = c[m] - (u0 * rows(c[m], j) + u1 * rows(c[m], j + 1))
            fix = 2.0 * one_at(((lane == k) & (sub == j)) | ((lane == k + 1) & (sub == j + 1)))
            r = (r - fix) - (u0 * (rows(r, j) - one_at(lane == k)) + u1 * (rows(r, j + 1) - one_at(lane == k + 1)))
        w = r + one_at(lane - 8 * q == sub)
        w_rows = [rows(w, m) for m in range(8)]
        base = groups // 2 if q < groups // 2 else 0
        update = lax.dot_general(
            a[q][:, 8 * base : 8 * base + size // 2],
            w,
            (((0,), (0,)), ((), ())),
            precision=lax.Precision.HIGHEST,
            preferred_element_type=f32,
        )
        for i in [i % groups for i in range(q + 1, q + groups)]:
            x = a[i]
            at = 8 * (i - base)
            if 0 <= at < size // 2 and i != q + 1:
                a[i] = x - update[at : at + 8, :]
            else:
                t = [lanes(x, 8 * q + m) * w_rows[m] for m in range(8)]
                a[i] = x - (((t[0] + t[1]) + (t[2] + t[3])) + ((t[4] + t[5]) + (t[6] + t[7])))
        a[q] = r
    return a


def exact_dot(a, b):
    return jnp.dot(a, b, precision=lax.Precision.HIGHEST, preferred_element_type=f32)


def solve_kernel(mine, other, targets_ref, z_ref, coef_ref, res_ref, dir_ref):
    size = mine.shape[1]
    gram = mine[0] + other[0]
    mix_t = mine[1] + other[1]
    quad = mine[2] + other[2]
    diag = ridge_weight + kernel_gain
    mix = mix_t.T
    both = mix + mix_t
    half_gain = 0.5 * kernel_gain
    sym = diag * gram + half_gain * both
    outer = (diag * diag) * gram + (diag * kernel_gain) * both + (kernel_gain * kernel_gain) * quad
    curv = diag * gram + kernel_gain * mix
    eye = lax.broadcasted_iota(jnp.int32, (size, size), 0) == lax.broadcasted_iota(jnp.int32, (size, size), 1)
    on_diag = jnp.where(eye, sym, 0.0)
    by_col = lax.rsqrt(jnp.sum(on_diag, axis=0, keepdims=True))
    by_row = lax.rsqrt(jnp.sum(on_diag, axis=1, keepdims=True))
    unit = sym * by_row * by_col
    parts = negated_inverse([unit[8 * i : 8 * i + 8, :] for i in range(size // 8)], size)
    minus_inverse = jnp.concatenate(parts, axis=0) * by_row * by_col
    step_t = -exact_dot(gram, minus_inverse)
    correction_t = exact_dot(curv - exact_dot(step_t, outer), minus_inverse)
    targets = targets_ref[...]
    image = ridge_weight * targets + kernel_gain * (targets.astype(bf16).astype(f32) + z_ref[...])
    residual = targets - exact_dot(step_t, image)
    coef_ref[...] = exact_dot(step_t, targets)
    res_ref[...] = residual
    dir_ref[...] = residual + exact_dot(correction_t, targets)


def flips(size, bit):
    return [(i, i ^ bit) for i in range(size)]


def call(kernel, out_shape, scratch_shapes, operands, limit):
    vmem = pl.BlockSpec(memory_space=pltpu.VMEM)
    return pl.pallas_call(
        kernel,
        out_shape=out_shape,
        in_specs=[vmem] * len(operands),
        out_specs=jax.tree.map(lambda _: vmem, out_shape),
        scratch_shapes=scratch_shapes,
        compiler_params=pltpu.CompilerParams(vmem_limit_bytes=limit),
    )(*operands)


def local(row_size, col_size):
    def run(features, targets):
        return step(features, targets)

    def step(features, targets):
        feat_rows, block = features.shape
        out_rows = targets.shape[0]
        scale = sharpness / feat_rows
        inner_rows = feat_rows + 16

        def flip(axis, bit):
            size = row_size if axis == "row" else col_size

            def send(x):
                return lax.ppermute(x, axis, flips(size, bit))

            return send

        def over_x(x):
            return flip("row", 1)(x)

        def over_y(x):
            return flip("col", col_size // 2)(x)

        def partner(x):
            return flip("col", 1)(x)

        def join(*pieces):
            return jnp.concatenate(pieces, axis=0)

        hops = [("row", 1 << s) for s in reversed(range(1, row_size.bit_length() - 1))]
        hops += [("col", 1 << s) for s in reversed(range(1, col_size.bit_length() - 2))]
        line = join(features, targets.astype(bf16))[None]
        for axis, bit in hops:
            line = join(line, flip(axis, bit)(line))
        half = line.shape[0] // 2
        early_y, early_x = over_y(line[:half]), over_x(line[:half])
        late_x, late_y = over_x(line[half:]), over_y(line[half:])
        far_x = over_x(early_y)
        near = join(early_x, late_x, early_y)
        other_near = partner(join(line, near))
        far = join(far_x, late_y, over_y(late_x))
        other_far = partner(far)

        limit = product_vmem if line.shape[0] <= 4 else None

        def stage(row_count, count):
            return [
                ((row_count * block, inner_rows), bf16),
                ((inner_rows, count * block), bf16),
                ((out_rows, row_count * block), bf16),
            ]

        def sums_of(count):
            return ((out_rows, count * block), f32)

        def shapes(entries):
            return tuple(jax.ShapeDtypeStruct(*x) for x in entries)

        n0, n1, n2 = line.shape[0], near.shape[0], far.shape[0]
        left0, right0, panel0, y0 = call(
            first_kernel(feat_rows, scale), shapes(stage(n0, n0) + [sums_of(n0)]), [], [line], limit
        )
        left1, right1, panel1, y0, y1 = call(
            second_kernel(feat_rows, scale),
            shapes(stage(n0 + 2 * n1, n1) + [sums_of(n0), sums_of(n1)]),
            [],
            [near, other_near, left0, right0, panel0, y0],
            limit,
        )
        full_left, right_shape, full_panel = stage(2 * n2, n2)
        own_left = ((n2 * block, inner_rows), bf16)
        own_panel = ((out_rows, n2 * block), bf16)
        left2, right2, panel2, y2 = call(
            cover_kernel(feat_rows, scale),
            shapes([own_left, right_shape, own_panel, sums_of(n2)]),
            [],
            [far, left0, panel0, left1, panel1],
            limit,
        )
        z, grams = call(
            third_kernel(feat_rows, scale),
            shapes([((out_rows, block), f32), ((3, out_rows, out_rows), f32)]),
            [pltpu.VMEM(*x) for x in [full_left, full_panel, ((2 * out_rows, 2 * out_rows), f32)]],
            [other_far, left2, right2, panel2, right0, panel0, right1, panel1, y0, y1, y2],
            limit,
        )
        return call(
            solve_kernel,
            tuple(jax.ShapeDtypeStruct(targets.shape, f32) for _ in range(3)),
            [],
            [grams, partner(grams), targets, z],
            solve_vmem,
        )

    return run


def solution(mesh):
    spec = P(None, ("col", "row"))
    return jax.shard_map(
        local(mesh.shape["row"], mesh.shape["col"]),
        mesh=mesh,
        in_specs=(spec, spec),
        out_specs=(spec, spec, spec),
        check_vma=False,
    )
```
